32 devices in a mesh: dp: 16 (over z, x, core), tensor: 2 (over y).
Axes of the slice: x: 2, y: 2, z: 4, core: 2. Of those that a mesh axis runs over, the one named last changes fastest.
Arguments:
- block_input: float32 [16384, 768], P('dp'), may hold values from -6 to 6
- gain_attn: float32 [768], replicated, may hold values from 0.1 to 1.9
- bias_attn: float32 [768], replicated, may hold values from -3 to 3
- gain_mlp: float32 [768], replicated, may hold values from 0.1 to 1.9
- bias_mlp: float32 [768], replicated, may hold values from -3 to 3
- qkv_weight: bfloat16 [768, 3, 768], P(None, None, 'tensor'), may hold values from -0.21875 to 0.21875
- qkv_bias: float32 [3, 768], P(None, 'tensor'), may hold values from -3 to 3
- out_weight: bfloat16 [768, 768], P('tensor'), may hold values from -1.75 to 1.75
- out_bias: float32 [768], replicated, may hold values from -3 to 3
- up_weight: bfloat16 [768, 3072], P(None, 'tensor'), may hold values from -0.21875 to 0.21875
- up_bias: float32 [3072], P('tensor'), may hold values from -3 to 3
- down_weight: bfloat16 [3072, 768], P('tensor'), may hold values from -0.109375 to 0.109375
- down_bias: float32 [768], replicated, may hold values from -3 to 3
- out_grad: float32 [16384, 768], P('dp'), may hold values from -6 to 6
Outputs:
- block_output: float32 [16384, 768], P('dp')
- input_grad: float32 [16384, 768], P('dp')
- grad_gain_attn: float32 [768], replicated
- grad_bias_attn: float32 [768], replicated
- grad_gain_mlp: float32 [768], replicated
- grad_bias_mlp: float32 [768], replicated
- grad_qkv_weight: float32 [768, 3, 768], P(None, None, 'tensor')
- grad_qkv_bias: float32 [3, 768], P(None, 'tensor')
- grad_out_weight: float32 [768, 768], P('tensor')
- grad_out_bias: float32 [768], replicated
- grad_up_weight: float32 [768, 3072], P(None, 'tensor')
- grad_up_bias: float32 [3072], P('tensor')
- grad_down_weight: float32 [3072, 768], P('tensor')
The draws below stay inside these ranges and needn't reach their ends.
All inputs are finite; a program needn't handle non-finite values.
Results may differ from the reference program's by a relative error of at most 0.013.
The reference program's roundings to bfloat16 on the way count: a program that leaves them out, or rounds other values in their place, can miss the bound.
Values sent between devices are 32-bit elements; how exact they have to be, the bound alone decides.
No kernel may reach another device: no remote copies, remote signals or barrier semaphores. Data moves between devices by JAX's collectives and lax.ppermute only.
A program may use at most 192 MiB of HBM per device.

```python
import math
import jax
import jax.numpy as jnp
from jax import lax

D = 768
HEADS = 12
HD = 64
FF = 3072
ROT = 16
L = 1024
TOKENS = 16384


def level_of(stream_key, extent, cuts, smallest, top_value):
    loudness, own = 1.0, jax.random.fold_in(stream_key, 6)
    for axis_at, parts in cuts:
        steps = jnp.exp(jax.random.uniform(jax.random.fold_in(own, axis_at), (parts,), jnp.float32, smallest / len(cuts), top_value / len(cuts)))
        loudness = loudness * jnp.repeat(steps, extent[axis_at] // parts).reshape([-1 if axis == axis_at else 1 for axis in range(len(extent))])
    return loudness


def bell_draw(key, extent, width, limit, cuts=(), kind=jnp.bfloat16):
    level = level_of(key, extent, cuts, -0.22, 0.18) if cuts else 1.0
    values = jax.random.normal(key, extent, jnp.float32) * width * level
    return jnp.minimum(jnp.maximum(values, -limit), limit).astype(kind)


def setup_inputs(seed: int = 0) -> dict:
    key_list = jax.random.split(jax.random.key(seed), 15)
    return {
        "block_input": bell_draw(key_list[0], (TOKENS, D), 1.0, 6.0, ((0, 16),), jnp.float32),
        "gain_attn": jnp.clip(1.0 + 0.18 * jax.random.normal(key_list[1], (D,), jnp.float32), 0.1, 1.9),
        "bias_attn": bell_draw(key_list[2], (D,), 0.5, 3.0, (), jnp.float32),
        "gain_mlp": jnp.clip(1.0 + 0.18 * jax.random.normal(key_list[3], (D,), jnp.float32), 0.1, 1.9),
        "bias_mlp": bell_draw(key_list[4], (D,), 0.5, 3.0, (), jnp.float32),
        "qkv_weight": bell_draw(key_list[5], (D, 3, HEADS * HD), D ** -0.5, 0.21875, ((2, 2),)),
        "qkv_bias": bell_draw(key_list[6], (3, HEADS * HD), 0.5, 3.0, ((1, 2),), jnp.float32),
        "out_weight": bell_draw(key_list[7], (HEADS * HD, D), (HEADS * HD // 64) ** -0.5, 1.75, ((0, 2),)),
        "out_bias": bell_draw(key_list[8], (D,), 0.5, 3.0, (), jnp.float32),
        "up_weight": bell_draw(key_list[9], (D, FF), D ** -0.5, 0.21875, ((1, 2),)),
        "up_bias": bell_draw(key_list[10], (FF,), 0.5, 3.0, ((0, 2),), jnp.float32),
        "down_weight": bell_draw(key_list[11], (FF, D), FF ** -0.5, 0.109375, ((0, 2),)),
        "down_bias": bell_draw(key_list[12], (D,), 0.5, 3.0, (), jnp.float32),
        "out_grad": bell_draw(key_list[13], (TOKENS, D), 1.0, 6.0, ((0, 16),), jnp.float32),
    }


EPSILON = 1e-05
SQRT_HALF = 0.7071067811865476
INV_ROOT_TAU = 0.3989422804014327
NEG_LARGE = -1e+30

def product(form, left, right):
    return jnp.einsum(form, left.astype(jnp.float32), right.astype(jnp.float32))

def gelu_pair(pre_act):
    normal_cdf = 0.5 * (1.0 + lax.erf(pre_act * SQRT_HALF))
    return (pre_act * normal_cdf, normal_cdf + pre_act * jnp.exp(-0.5 * pre_act * pre_act) * INV_ROOT_TAU)

def rotary_tables(length):
    halfrot = ROT // 2
    frequency = jnp.exp(jnp.arange(halfrot, dtype=jnp.float32) * (-2.0 * math.log(10000.0) / ROT))
    angles = jnp.arange(length, dtype=jnp.float32)[:, None] * frequency[None, :]
    return (jnp.cos(angles)[:, None, :], jnp.sin(angles)[:, None, :])

def rotate(values, cosine, sine_table, direction):
    halfrot = ROT // 2
    first_half = values[..., :halfrot]
    second_half = values[..., halfrot:ROT]
    turned_one = first_half * cosine - direction * second_half * sine_table
    turned_two = second_half * cosine + direction * first_half * sine_table
    return jnp.concatenate([turned_one, turned_two, values[..., ROT:]], axis=-1)

def masked_scores(query_blk, keys_all, first_row):
    length = keys_all.shape[0]
    block_rows = query_blk.shape[0]
    scores = product('qhd,khd->hqk', query_blk, keys_all) * HD ** (-0.5)
    causal = jnp.arange(length)[None, :] <= (first_row + jnp.arange(block_rows))[:, None]
    return jnp.where(causal[None], scores, NEG_LARGE)

def attend(queries, keys_all, values_all):
    length = queries.shape[0]
    block_rows = min(512, length)
    outputs = []
    totals = []
    for first_row in range(0, length, block_rows):
        scores = masked_scores(queries[first_row:first_row + block_rows], keys_all, first_row)
        row_max = lax.optimization_barrier(jnp.max(scores, axis=-1, keepdims=True))
        log_total = row_max + jnp.log(lax.optimization_barrier(jnp.sum(jnp.exp(scores - row_max), axis=-1, keepdims=True)))
        soft_weights = jnp.exp(scores - log_total).astype(jnp.bfloat16)
        outputs.append(product('hqk,khd->qhd', soft_weights, values_all).astype(jnp.bfloat16))
        totals.append(log_total[..., 0])
    return (jnp.concatenate(outputs, 0), jnp.concatenate(totals, 1))

def attend_back(queries, keys_all, values_all, attended, att_grad, log_totals):
    length = queries.shape[0]
    block_rows = min(512, length)
    key_grad = jnp.zeros(keys_all.shape, jnp.float32)
    value_grad = jnp.zeros(values_all.shape, jnp.float32)
    query_grads = []
    for first_row in range(0, length, block_rows):
        query_blk = queries[first_row:first_row + block_rows]
        grad_blk = att_grad[first_row:first_row + block_rows]
        out_blk = attended[first_row:first_row + block_rows]
        delta_blk = lax.optimization_barrier(jnp.sum(grad_blk.astype(jnp.float32) * out_blk.astype(jnp.float32), axis=-1))
        scores = masked_scores(query_blk, keys_all, first_row)
        soft_full = jnp.exp(scores - log_totals[:, first_row:first_row + block_rows, None])
        soft_weights = soft_full.astype(jnp.bfloat16)
        value_grad = value_grad + product('hqk,qhd->khd', soft_weights, grad_blk)
        weight_grad = product('qhd,khd->hqk', grad_blk, values_all)
        score_grad = (soft_full * (weight_grad - delta_blk.T[:, :, None]) * HD ** (-0.5)).astype(jnp.bfloat16)
        query_grads.append(product('hqk,khd->qhd', score_grad, keys_all))
        key_grad = key_grad + product('hqk,qhd->khd', score_grad, query_blk)
    return (jnp.concatenate(query_grads, 0), key_grad, value_grad)

def norm_back(grad_norm, gain, normed, inv_std):
    scaled = grad_norm * gain
    return inv_std * (scaled - lax.optimization_barrier(jnp.mean(scaled, axis=-1, keepdims=True)) - normed * lax.optimization_barrier(jnp.mean(scaled * normed, axis=-1, keepdims=True)))

def one_sequence(seq_input, seq_grad, params):
    gain_attn, bias_attn, gain_mlp, bias_mlp, qkv_weight, qkv_bias, out_weight, out_bias, up_weight, up_bias, down_weight, down_bias = params
    length = seq_input.shape[0]
    inner = HEADS * HD
    row_mean = lax.optimization_barrier(jnp.mean(seq_input, axis=-1, keepdims=True))
    centered = seq_input - row_mean
    inv_std = lax.rsqrt(lax.optimization_barrier(jnp.mean(centered * centered, axis=-1, keepdims=True)) + EPSILON)
    normed = centered * inv_std
    attn_in = (normed * gain_attn + bias_attn).astype(jnp.bfloat16)
    mlp_in = (normed * gain_mlp + bias_mlp).astype(jnp.bfloat16)
    flat_qkv = qkv_weight.reshape(D, 3 * inner)
    projected = jnp.dot(attn_in, flat_qkv, preferred_element_type=jnp.float32).reshape(length, 3, inner) + qkv_bias
    cosine, sine_table = rotary_tables(length)
    queries = rotate(projected[:, 0].reshape(length, HEADS, HD), cosine, sine_table, 1.0).astype(jnp.bfloat16)
    keys_all = rotate(projected[:, 1].reshape(length, HEADS, HD), cosine, sine_table, 1.0).astype(jnp.bfloat16)
    values_all = projected[:, 2].reshape(length, HEADS, HD).astype(jnp.bfloat16)
    attended, log_totals = attend(queries, keys_all, values_all)
    att_flat = attended.reshape(length, inner)
    pre_act = jnp.dot(mlp_in, up_weight, preferred_element_type=jnp.float32) + up_bias
    activated, slope = gelu_pair(pre_act)
    act_half = activated.astype(jnp.bfloat16)
    branches = jnp.dot(att_flat, out_weight, preferred_element_type=jnp.float32) + jnp.dot(act_half, down_weight, preferred_element_type=jnp.float32)
    block_output = seq_input + branches + out_bias + down_bias
    grad_half = seq_grad.astype(jnp.bfloat16)
    grad_bias_out = lax.optimization_barrier(jnp.sum(seq_grad, axis=0))
    grad_out_w = jnp.dot(att_flat.T, grad_half, preferred_element_type=jnp.float32)
    grad_down_w = jnp.dot(act_half.T, grad_half, preferred_element_type=jnp.float32)
    att_grad = jnp.dot(grad_half, out_weight.T, preferred_element_type=jnp.float32).astype(jnp.bfloat16)
    att_grad = att_grad.reshape(length, HEADS, HD)
    pre_grad = jnp.dot(grad_half, down_weight.T, preferred_element_type=jnp.float32) * slope
    grad_up_b = lax.optimization_barrier(jnp.sum(pre_grad, axis=0))
    pre_half = pre_grad.astype(jnp.bfloat16)
    grad_up_w = jnp.dot(mlp_in.T, pre_half, preferred_element_type=jnp.float32)
    mlp_norm_grad = jnp.dot(pre_half, up_weight.T, preferred_element_type=jnp.float32)
    query_grad, key_grad, value_grad = attend_back(queries, keys_all, values_all, attended, att_grad, log_totals)
    query_back = rotate(query_grad, cosine, sine_table, -1.0).reshape(length, inner)
    key_back = rotate(key_grad, cosine, sine_table, -1.0).reshape(length, inner)
    proj_grad = jnp.stack([query_back, key_back, value_grad.reshape(length, inner)], axis=1)
    grad_qkv_b = lax.optimization_barrier(jnp.sum(proj_grad, axis=0))
    proj_half = proj_grad.astype(jnp.bfloat16).reshape(length, 3 * inner)
    grad_qkv_w = jnp.dot(attn_in.T, proj_half, preferred_element_type=jnp.float32).reshape(D, 3, inner)
    attn_norm_grad = jnp.dot(proj_half, flat_qkv.T, preferred_element_type=jnp.float32)
    grad_gain_a = lax.optimization_barrier(jnp.sum(attn_norm_grad * normed, axis=0))
    grad_bias_a = lax.optimization_barrier(jnp.sum(attn_norm_grad, axis=0))
    grad_gain_m = lax.optimization_barrier(jnp.sum(mlp_norm_grad * normed, axis=0))
    grad_bias_m = lax.optimization_barrier(jnp.sum(mlp_norm_grad, axis=0))
    input_grad = seq_grad + norm_back(attn_norm_grad, gain_attn, normed, inv_std) + norm_back(mlp_norm_grad, gain_mlp, normed, inv_std)
    return (block_output, input_grad, (grad_gain_a, grad_bias_a, grad_gain_m, grad_bias_m, grad_qkv_w, grad_qkv_b, grad_out_w, grad_bias_out, grad_up_w, grad_up_b, grad_down_w))

def reference(block_input, gain_attn, bias_attn, gain_mlp, bias_mlp, qkv_weight, qkv_bias, out_weight, out_bias, up_weight, up_bias, down_weight, down_bias, out_grad):
    params = (gain_attn, bias_attn, gain_mlp, bias_mlp, qkv_weight, qkv_bias, out_weight, out_bias, up_weight, up_bias, down_weight, down_bias)
    count = TOKENS // L
    inner = HEADS * HD
    initial = (jnp.zeros((D,), jnp.float32), jnp.zeros((D,), jnp.float32), jnp.zeros((D,), jnp.float32), jnp.zeros((D,), jnp.float32), jnp.zeros((D, 3, inner), jnp.float32), jnp.zeros((3, inner), jnp.float32), jnp.zeros((inner, D), jnp.float32), jnp.zeros((D,), jnp.float32), jnp.zeros((D, FF), jnp.float32), jnp.zeros((FF,), jnp.float32), jnp.zeros((FF, D), jnp.float32))

    def advance(carry, pair):
        result, back, grads = one_sequence(pair[0], pair[1], params)
        return (tuple((running + adding for running, adding in zip(carry, grads))), (result, back))
    sums, (outputs, backs) = lax.scan(advance, initial, (block_input.reshape(count, L, D), out_grad.reshape(count, L, D)))
    return (outputs.reshape(TOKENS, D), backs.reshape(TOKENS, D), sums[0], sums[1], sums[2], sums[3], sums[4], sums[5], sums[6], sums[7], sums[8], sums[9], sums[10])
```

```python
import math

import jax
import jax.numpy as jnp
from jax import lax
from jax.sharding import PartitionSpec as P

D = 768
HD = 64
ROT = 16
L = 1024


EPSILON = 1e-05
SQRT_HALF = 0.7071067811865476
INV_ROOT_TAU = 0.3989422804014327
NEG_LARGE = -1e30


def gelu_pair(pre_act):
    normal_cdf = 0.5 * (1.0 + lax.erf(pre_act * SQRT_HALF))
    return (
        pre_act * normal_cdf,
        normal_cdf + pre_act * jnp.exp(-0.5 * pre_act * pre_act) * INV_ROOT_TAU,
    )


def rotary_tables(length):
    halfrot = ROT // 2
    frequency = jnp.exp(jnp.arange(halfrot, dtype=jnp.float32) * (-2.0 * math.log(10000.0) / ROT))
    angles = jnp.arange(length, dtype=jnp.float32)[:, None] * frequency[None, :]
    return (jnp.cos(angles)[:, None, :], jnp.sin(angles)[:, None, :])


def rotate(values, cosine, sine_table, direction):
    halfrot = ROT // 2
    first_half = values[..., :halfrot]
    second_half = values[..., halfrot:ROT]
    turned_one = first_half * cosine - direction * second_half * sine_table
    turned_two = second_half * cosine + direction * first_half * sine_table
    return jnp.concatenate([turned_one, turned_two, values[..., ROT:]], axis=-1)


def masked_scores(query_blk, keys_all, first_row):
    length = keys_all.shape[0]
    block_rows = query_blk.shape[0]
    scores = jnp.einsum(
        "qhd,khd->hqk", query_blk, keys_all, preferred_element_type=jnp.float32
    ) * HD ** (-0.5)
    causal = jnp.arange(length)[None, :] <= (first_row + jnp.arange(block_rows))[:, None]
    return jnp.where(causal[None], scores, NEG_LARGE)


def attend(queries, keys_all, values_all):
    length = queries.shape[0]
    block_rows = min(512, length)
    outputs = []
    totals = []
    for first_row in range(0, length, block_rows):
        scores = masked_scores(queries[first_row : first_row + block_rows], keys_all, first_row)
        row_max = jnp.max(scores, axis=-1, keepdims=True)
        log_total = row_max + jnp.log(jnp.sum(jnp.exp(scores - row_max), axis=-1, keepdims=True))
        soft_weights = jnp.exp(scores - log_total).astype(jnp.bfloat16)
        outputs.append(
            jnp.einsum(
                "hqk,khd->qhd", soft_weights, values_all, preferred_element_type=jnp.float32
            ).astype(jnp.bfloat16)
        )
        totals.append(log_total[..., 0])
    return (jnp.concatenate(outputs, 0), jnp.concatenate(totals, 1))


def attend_back(queries, keys_all, values_all, attended, att_grad, log_totals):
    length = queries.shape[0]
    block_rows = min(512, length)
    key_grad = jnp.zeros(keys_all.shape, jnp.float32)
    value_grad = jnp.zeros(values_all.shape, jnp.float32)
    query_grads = []
    for first_row in range(0, length, block_rows):
        query_blk = queries[first_row : first_row + block_rows]
        grad_blk = att_grad[first_row : first_row + block_rows]
        out_blk = attended[first_row : first_row + block_rows]
        delta_blk = jnp.sum(grad_blk.astype(jnp.float32) * out_blk.astype(jnp.float32), axis=-1)
        scores = masked_scores(query_blk, keys_all, first_row)
        soft_full = jnp.exp(scores - log_totals[:, first_row : first_row + block_rows, None])
        soft_weights = soft_full.astype(jnp.bfloat16)
        value_grad = value_grad + jnp.einsum(
            "hqk,qhd->khd", soft_weights, grad_blk, preferred_element_type=jnp.float32
        )
        weight_grad = jnp.einsum(
            "qhd,khd->hqk", grad_blk, values_all, preferred_element_type=jnp.float32
        )
        score_grad = (soft_full * (weight_grad - delta_blk.T[:, :, None]) * HD ** (-0.5)).astype(
            jnp.bfloat16
        )
        query_grads.append(
            jnp.einsum("hqk,khd->qhd", score_grad, keys_all, preferred_element_type=jnp.float32)
        )
        key_grad = key_grad + jnp.einsum(
            "hqk,qhd->khd", score_grad, query_blk, preferred_element_type=jnp.float32
        )
    return (jnp.concatenate(query_grads, 0), key_grad, value_grad)


def token_contract(left, right):
    return lax.dot_general(
        left, right, (((0,), (0,)), ((), ())), preferred_element_type=jnp.float32
    )


def flip(axis, size, mask):
    return [(place, place ^ mask) for place in range(size)]


def give_half(rows, bit, axis, perm):
    half = rows.shape[0] // 2
    sent = lax.dynamic_slice_in_dim(rows, (1 - bit) * half, half, 0)
    kept = lax.dynamic_slice_in_dim(rows, bit * half, half, 0)
    return kept + lax.ppermute(sent, axis, perm)


def join_half(rows, bit, axis, perm):
    half = rows.shape[0]
    other = lax.ppermute(rows, axis, perm)
    whole = jnp.zeros((2 * half,) + rows.shape[1:], rows.dtype)
    whole = lax.dynamic_update_slice_in_dim(whole, rows, bit * half, 0)
    return lax.dynamic_update_slice_in_dim(whole, other, (1 - bit) * half, 0)


def sum_over_dp(rows, order):
    size = lax.axis_size("dp")
    place = lax.axis_index("dp")
    stages = [((place >> k) & 1, "dp", flip("dp", size, 1 << k)) for k in order]
    for stage in stages:
        rows = give_half(rows, *stage)
    for stage in reversed(stages):
        rows = join_half(rows, *stage)
    return rows


def small_sum_over_dp(rows):
    size = lax.axis_size("dp")
    step = 1
    while step < size:
        rows = rows + lax.ppermute(rows, "dp", flip("dp", size, step))
        step *= 2
    return rows


def from_partner(rows):
    return lax.ppermute(rows, "tensor", flip("tensor", lax.axis_size("tensor"), 1))


def on_device(
    block_input,
    gain_attn,
    bias_attn,
    gain_mlp,
    bias_mlp,
    qkv_weight,
    qkv_bias,
    out_weight,
    out_bias,
    up_weight,
    up_bias,
    down_weight,
    down_bias,
    out_grad,
):
    rows_here = block_input.shape[0]
    seq_here = rows_here // L
    inner = qkv_weight.shape[2]
    heads_here = inner // HD
    row_mean = jnp.mean(block_input, axis=-1, keepdims=True)
    centered = block_input - row_mean
    inv_std = lax.rsqrt(jnp.mean(centered * centered, axis=-1, keepdims=True) + EPSILON)
    normed = centered * inv_std
    attn_in = (normed * gain_attn + bias_attn).astype(jnp.bfloat16)
    mlp_in = (normed * gain_mlp + bias_mlp).astype(jnp.bfloat16)
    flat_qkv = qkv_weight.reshape(D, 3 * inner)
    projected = (
        jnp.dot(attn_in, flat_qkv, preferred_element_type=jnp.float32).reshape(rows_here, 3, inner)
        + qkv_bias
    )
    cosine, sine_table = rotary_tables(L)
    queries = rotate(
        projected[:, 0].reshape(seq_here, L, heads_here, HD), cosine, sine_table, 1.0
    ).astype(jnp.bfloat16)
    keys_all = rotate(
        projected[:, 1].reshape(seq_here, L, heads_here, HD), cosine, sine_table, 1.0
    ).astype(jnp.bfloat16)
    values_all = projected[:, 2].reshape(seq_here, L, heads_here, HD).astype(jnp.bfloat16)
    seq_index = 0
    attended_seq, totals_seq = attend(
        queries[seq_index], keys_all[seq_index], values_all[seq_index]
    )
    attended_list = [attended_seq]
    totals_list = [totals_seq]
    att_flat = jnp.stack(attended_list, 0).reshape(rows_here, inner)
    pre_act = jnp.dot(mlp_in, up_weight, preferred_element_type=jnp.float32) + up_bias
    activated, slope = gelu_pair(pre_act)
    act_half = activated.astype(jnp.bfloat16)
    branches = jnp.dot(att_flat, out_weight, preferred_element_type=jnp.float32) + jnp.dot(
        act_half, down_weight, preferred_element_type=jnp.float32
    )
    summed = branches + from_partner(branches)
    block_output = block_input + summed + out_bias + down_bias
    grad_half = out_grad.astype(jnp.bfloat16)
    grad_bias_out = jnp.sum(out_grad, axis=0)
    grad_out_w = token_contract(att_flat, grad_half)
    grad_down_w = token_contract(act_half, grad_half)
    att_grad = jnp.dot(grad_half, out_weight.T, preferred_element_type=jnp.float32).astype(
        jnp.bfloat16
    )
    att_grad = att_grad.reshape(seq_here, L, heads_here, HD)
    pre_grad = jnp.dot(grad_half, down_weight.T, preferred_element_type=jnp.float32) * slope
    grad_up_b = jnp.sum(pre_grad, axis=0)
    pre_half = pre_grad.astype(jnp.bfloat16)
    grad_up_w = token_contract(mlp_in, pre_half)
    mlp_part = jnp.dot(pre_half, up_weight.T, preferred_element_type=jnp.float32)
    seq_index = 0
    query_grad, key_grad, value_grad = attend_back(
        queries[seq_index],
        keys_all[seq_index],
        values_all[seq_index],
        attended_list[seq_index],
        att_grad[seq_index],
        totals_list[seq_index],
    )
    query_list = [query_grad]
    key_list = [key_grad]
    value_list = [value_grad]
    query_back = rotate(jnp.stack(query_list, 0), cosine, sine_table, -1.0).reshape(
        rows_here, inner
    )
    key_back = rotate(jnp.stack(key_list, 0), cosine, sine_table, -1.0).reshape(rows_here, inner)
    value_back = jnp.stack(value_list, 0).reshape(rows_here, inner)
    proj_grad = jnp.stack([query_back, key_back, value_back], axis=1)
    grad_qkv_b = jnp.sum(proj_grad, axis=0)
    proj_half = proj_grad.astype(jnp.bfloat16).reshape(rows_here, 3 * inner)
    grad_qkv_w = token_contract(attn_in, proj_half).reshape(D, 3, inner)
    attn_part = jnp.dot(proj_half, flat_qkv.T, preferred_element_type=jnp.float32)
    shared = attn_part * gain_attn + mlp_part * gain_mlp
    shared = shared + from_partner(shared)
    input_grad = out_grad + inv_std * (
        shared
        - jnp.mean(shared, axis=-1, keepdims=True)
        - normed * jnp.mean(shared * normed, axis=-1, keepdims=True)
    )
    norm_sums = jnp.stack(
        [
            jnp.sum(attn_part * normed, axis=0),
            jnp.sum(attn_part, axis=0),
            jnp.sum(mlp_part * normed, axis=0),
            jnp.sum(mlp_part, axis=0),
        ]
    )
    norm_sums = norm_sums + from_partner(norm_sums)
    small = jnp.concatenate(
        [norm_sums.reshape(-1), grad_qkv_b.reshape(-1), grad_up_b, grad_bias_out]
    ).reshape(-1, 128)
    small = small_sum_over_dp(small).reshape(-1)
    bits = lax.axis_size("dp").bit_length() - 1
    near = list(range(bits))
    far = [0] + ([2, 1] + list(range(3, bits)) if bits > 2 else near[1:])
    grad_up_w = sum_over_dp(grad_up_w, near)
    grad_down_w = sum_over_dp(grad_down_w, far)
    grad_qkv_w = sum_over_dp(grad_qkv_w.reshape(D, 3 * inner), near).reshape(D, 3, inner)
    grad_out_w = sum_over_dp(grad_out_w, far)
    grad_gain_a, grad_bias_a, grad_gain_m, grad_bias_m = jnp.split(small[: 4 * D], 4)
    at = 4 * D
    grad_qkv_b = small[at : at + 3 * inner].reshape(3, inner)
    at += 3 * inner
    grad_up_b = small[at : at + grad_up_b.shape[0]]
    grad_bias_out = small[at + grad_up_b.shape[0] :]
    return (
        block_output,
        input_grad,
        grad_gain_a,
        grad_bias_a,
        grad_gain_m,
        grad_bias_m,
        grad_qkv_w,
        grad_qkv_b,
        grad_out_w,
        grad_bias_out,
        grad_up_w,
        grad_up_b,
        grad_down_w,
    )


def solution(mesh):
    in_specs = (
        P("dp", None),
        P(),
        P(),
        P(),
        P(),
        P(None, None, "tensor"),
        P(None, "tensor"),
        P("tensor", None),
        P(),
        P(None, "tensor"),
        P("tensor"),
        P("tensor", None),
        P(),
        P("dp", None),
    )
    out_specs = (
        P("dp", None),
        P("dp", None),
        P(),
        P(),
        P(),
        P(),
        P(None, None, "tensor"),
        P(None, "tensor"),
        P("tensor", None),
        P(),
        P(None, "tensor"),
        P("tensor"),
        P("tensor", None),
    )
    return jax.shard_map(
        on_device, mesh=mesh, in_specs=in_specs, out_specs=out_specs, check_vma=False
    )
```

```python
import functools
import math

import jax
import jax.numpy as jnp
from jax import lax
from jax.experimental import pallas as pl
from jax.experimental.pallas import tpu as pltpu
from jax.sharding import PartitionSpec as P

D = 768
HD = 64
ROT = 16
L = 1024
EPSILON = 1e-05
SQRT_HALF = 0.7071067811865476
INV_ROOT_TAU = 0.3989422804014327
NEG_LARGE = -1e30
BLOCK = 256
PAIR = 2 * HD
F32 = jnp.float32
BF16 = jnp.bfloat16
VMEM_BYTES = 60 * 1024 * 1024


def mm(left, right, left_dim, right_dim):
    return lax.dot_general(
        left, right, (((left_dim,), (right_dim,)), ((), ())), preferred_element_type=F32
    )


def call(kernel, grid, in_specs, out_specs, out_shape, scratch=(), flops=0, nbytes=0, prefetch=1):
    return pl.pallas_call(
        kernel,
        grid_spec=pltpu.PrefetchScalarGridSpec(
            num_scalar_prefetch=prefetch,
            grid=grid,
            in_specs=in_specs,
            out_specs=out_specs,
            scratch_shapes=scratch,
        ),
        out_shape=out_shape,
        compiler_params=pltpu.CompilerParams(
            dimension_semantics=("arbitrary",) * len(grid), vmem_limit_bytes=VMEM_BYTES
        ),
        cost_estimate=pl.CostEstimate(flops=flops, bytes_accessed=nbytes, transcendentals=0),
    )


def whole(shape):
    return pl.BlockSpec(shape, lambda *_: (0,) * len(shape), pipeline_mode=pl.Buffered(1))


def kept_out(shape):
    return pl.BlockSpec(shape, lambda *_: (0,) * len(shape))


def sds(shape, dtype=F32):
    return jax.ShapeDtypeStruct(shape, dtype)


def mlp_kernel(
    bit_ref, x_ref, og_ref, ga_ref, ba_ref, gm_ref, bm_ref, up_ref, upb_ref, down_ref,
    attn_in_ref, gh_ref, normed_ref, inv_ref, part_ref, em_ref, us_ref, uk_ref, ds_ref, dk_ref,
    ubg_ref, sums_ref, mlp_in_ref,
):
    step = pl.program_id(0)
    steps = pl.num_programs(0)
    rows = x_ref.shape[0]
    spans = [pl.ds(r, BLOCK) for r in range(0, rows, BLOCK)]

    @pl.when(step == 0)
    def _():
        total = jnp.zeros((1, D), F32)
        for span in spans:
            x = x_ref[span, :]
            centered = x - jnp.mean(x, axis=-1, keepdims=True)
            inv_std = lax.rsqrt(jnp.mean(centered * centered, axis=-1, keepdims=True) + EPSILON)
            normed = centered * inv_std
            normed_ref[span, :] = normed
            inv_ref[span, :] = inv_std
            attn_in_ref[span, :] = (normed * ga_ref[...] + ba_ref[...]).astype(BF16)
            mlp_in_ref[span, :] = (normed * gm_ref[...] + bm_ref[...]).astype(BF16)
            grad = og_ref[span, :]
            total += jnp.sum(grad, axis=0, keepdims=True)
            gh_ref[span, :] = grad.astype(BF16)
        sums_ref[0:1, :] = total

    up = up_ref[...]
    down = down_ref[...]
    acts = []
    halves = []
    bias_total = jnp.zeros((1, up.shape[1]), F32)
    for span in spans:
        pre_act = mm(mlp_in_ref[span, :], up, 1, 0) + upb_ref[...]
        normal_cdf = 0.5 * (1.0 + lax.erf(pre_act * SQRT_HALF))
        slope = normal_cdf + pre_act * jnp.exp(-0.5 * pre_act * pre_act) * INV_ROOT_TAU
        act = (pre_act * normal_cdf).astype(BF16)
        acts.append(act)
        pre_grad = mm(gh_ref[span, :], down, 1, 1) * slope
        bias_total += jnp.sum(pre_grad, axis=0, keepdims=True)
        half = pre_grad.astype(BF16)
        halves.append(half)
        added = mm(act, down, 1, 0)
        back = mm(half, up, 1, 1)

        @pl.when(step == 0)
        def _():
            part_ref[span, :] = added
            em_ref[span, :] = back

        @pl.when(step > 0)
        def _():
            part_ref[span, :] += added
            em_ref[span, :] += back

    ubg_ref[...] = bias_total
    act = jnp.concatenate(acts, 0)
    half = jnp.concatenate(halves, 0)
    grad_down = mm(act, gh_ref[...], 0, 0)
    grad_up = mm(mlp_in_ref[...], half, 0, 0)

    @pl.when(step < steps // 2)
    def _():
        us_ref[...] = grad_up
        ds_ref[...] = grad_down

    @pl.when(step >= steps // 2)
    def _():
        uk_ref[...] = grad_up
        dk_ref[...] = grad_down

    @pl.when(step == steps - 1)
    def _():
        first = jnp.zeros((1, D), F32)
        second = jnp.zeros((1, D), F32)
        for span in spans:
            back = em_ref[span, :]
            first += jnp.sum(back * normed_ref[span, :], axis=0, keepdims=True)
            second += jnp.sum(back, axis=0, keepdims=True)
            em_ref[span, :] = back * gm_ref[...]
        sums_ref[1:2, :] = first
        sums_ref[2:3, :] = second
        sums_ref[3:8, :] = jnp.zeros((5, D), F32)


def mlp(bit, x, og, ga, ba, gm, bm, up, upb, down):
    rows = x.shape[0]
    hidden = up.shape[1]
    steps = hidden // BLOCK
    h = steps // 2

    def at(i, bit_ref):
        return lax.rem(i + (1 - bit_ref[0]) * h, steps)

    vec = whole((1, D))
    tall = (rows, D)
    first = lambda i: jnp.minimum(i, h - 1)
    last = lambda i: jnp.maximum(i - h, 0)
    return call(
        mlp_kernel,
        (steps,),
        [
            whole(tall), whole(tall), vec, vec, vec, vec,
            pl.BlockSpec((D, BLOCK), lambda i, b: (0, at(i, b))),
            pl.BlockSpec((1, BLOCK), lambda i, b: (0, at(i, b))),
            pl.BlockSpec((BLOCK, D), lambda i, b: (at(i, b), 0)),
        ],
        [
            kept_out(tall), kept_out(tall), kept_out(tall), kept_out((rows, 1)), kept_out(tall), kept_out(tall),
            pl.BlockSpec((D, BLOCK), lambda i, b: (0, first(i))),
            pl.BlockSpec((D, BLOCK), lambda i, b: (0, last(i))),
            pl.BlockSpec((BLOCK, D), lambda i, b: (first(i), 0)),
            pl.BlockSpec((BLOCK, D), lambda i, b: (last(i), 0)),
            pl.BlockSpec((1, BLOCK), lambda i, b: (0, at(i, b))),
            kept_out((8, D)),
        ],
        [
            sds(tall, BF16), sds(tall, BF16), sds(tall), sds((rows, 1)), sds(tall), sds(tall),
            sds((D, hidden // 2)), sds((D, hidden // 2)), sds((hidden // 2, D)), sds((hidden // 2, D)),
            sds((1, hidden)), sds((8, D)),
        ],
        [pltpu.VMEM(tall, BF16)],
        flops=12 * rows * D * hidden,
        nbytes=40_000_000,
    )(bit, x, og, ga, ba, gm, bm, up, upb, down)


def turn(values, cosine, sine, direction):
    low = lax.broadcasted_iota(jnp.int32, values.shape, 1) % HD < ROT // 2
    ahead = pltpu.roll(values, PAIR - ROT // 2, 1)
    behind = pltpu.roll(values, ROT // 2, 1)
    crossed = jnp.where(low, -ahead, behind)
    return values * cosine + direction * crossed * sine


def head_mask(head, shape):
    lane = lax.broadcasted_iota(jnp.int32, shape, 1)
    return lane < HD if head == 0 else lane >= HD


def forward_kernel(
    attn_in_ref, wq_ref, wk_ref, wv_ref, bq_ref, bk_ref, bv_ref, cos_ref, sin_ref, part_ref, out_ref,
    q_ref, k_ref, v_ref, att_ref, lse_ref, branch_ref,
    att_all,
):
    pair = pl.program_id(0)
    rows = attn_in_ref.shape[0]
    attn_in = attn_in_ref[...]
    cosine = cos_ref[...]
    sine = sin_ref[...]
    q_ref[...] = turn(mm(attn_in, wq_ref[...], 1, 0) + bq_ref[...], cosine, sine, 1.0).astype(BF16)
    k_ref[...] = turn(mm(attn_in, wk_ref[...], 1, 0) + bk_ref[...], cosine, sine, 1.0).astype(BF16)
    v_ref[...] = (mm(attn_in, wv_ref[...], 1, 0) + bv_ref[...]).astype(BF16)
    scale = jnp.asarray(HD**-0.5, BF16)
    for first in range(0, rows, BLOCK):
        span = pl.ds(first, BLOCK)
        length = first + BLOCK
        query = q_ref[span, :] * scale
        keys = k_ref[0:length, :]
        vals = v_ref[0:length, :]
        zero = jnp.zeros_like(query)
        row = lax.broadcasted_iota(jnp.int32, (BLOCK, length), 0) + first
        seen = lax.broadcasted_iota(jnp.int32, (BLOCK, length), 1) <= row
        results = []
        for head in range(2):
            mine = head_mask(head, query.shape)
            scores = mm(jnp.where(mine, query, zero), keys, 1, 1)
            scores = jnp.where(seen, scores, NEG_LARGE)
            top = jnp.max(scores, axis=-1, keepdims=True)
            weights = jnp.exp(scores - top)
            total = jnp.sum(weights, axis=-1, keepdims=True)
            lse_ref[0, span, head : head + 1] = top + jnp.log(total)
            soft = (weights * (1.0 / total)).astype(BF16)
            results.append(mm(soft, vals, 1, 0))
        att = jnp.where(head_mask(0, results[0].shape), results[0], results[1]).astype(BF16)
        att_ref[span, :] = att
        att_all[span, pl.ds(pl.multiple_of(pair * PAIR, PAIR), PAIR)] = att

    @pl.when(pair == pl.num_programs(0) - 1)
    def _():
        for first in range(0, rows, BLOCK):
            span = pl.ds(first, BLOCK)
            branch_ref[span, :] = part_ref[span, :] + mm(att_all[span, :], out_ref[...], 1, 0)


def slot_cols(slot, height):
    return pl.BlockSpec((None, height, PAIR), lambda i, *_: (slot, 0, i))


def attention_forward(attn_in, flat_qkv, flat_bias, cosine, sine, part, out_weight):
    rows = attn_in.shape[0]
    inner = out_weight.shape[0]
    pairs = inner // PAIR
    tall = (rows, D)
    lane = pl.BlockSpec((rows, PAIR), lambda i: (0, i))
    return call(
        forward_kernel,
        (pairs,),
        [whole(tall)]
        + [slot_cols(s, D) for s in range(3)]
        + [slot_cols(s, 1) for s in range(3)]
        + [whole((rows, PAIR)), whole((rows, PAIR)), whole(tall), whole((inner, D))],
        [lane, lane, lane, lane, pl.BlockSpec((1, rows, 2), lambda i: (i, 0, 0)), kept_out(tall)],
        [sds((rows, inner), BF16)] * 4 + [sds((pairs, rows, 2)), sds(tall)],
        [pltpu.VMEM((rows, inner), BF16)],
        flops=8 * rows * D * inner + 4 * rows * rows * inner,
        nbytes=20_000_000,
        prefetch=0,
    )(attn_in, flat_qkv, flat_qkv, flat_qkv, flat_bias, flat_bias, flat_bias, cosine, sine, part, out_weight)


def backward_kernel(
    bit_ref, attn_in_ref, wq_ref, wk_ref, wv_ref, cos_ref, sin_ref, out_ref, gh_ref, em_ref, normed_ref, ga_ref,
    q_ref, k_ref, v_ref, att_ref, lse_ref,
    e_ref, as_ref, ak_ref, bs_ref, bk_ref, qb_ref, sums_ref,
    dq_acc, dk_acc, dv_acc,
):
    pair = pl.program_id(0)
    rows = attn_in_ref.shape[0]
    half = D // 2
    grad_att = mm(gh_ref[...], out_ref[...], 1, 1).astype(BF16)
    product = grad_att.astype(F32) * att_ref[...].astype(F32)
    scale = jnp.asarray(HD**-0.5, BF16)
    for number, first in enumerate(range(0, rows, BLOCK)):
        span = pl.ds(first, BLOCK)
        length = first + BLOCK
        query = q_ref[span, :] * scale
        keys = k_ref[0:length, :]
        vals = v_ref[0:length, :]
        grads = grad_att[first : first + BLOCK, :]
        part = product[first : first + BLOCK, :]
        row = lax.broadcasted_iota(jnp.int32, (BLOCK, length), 0) + first
        seen = lax.broadcasted_iota(jnp.int32, (BLOCK, length), 1) <= row
        for head in range(2):
            mine = head_mask(head, query.shape)
            q_head = jnp.where(mine, query, jnp.zeros_like(query))
            g_head = jnp.where(mine, grads, jnp.zeros_like(grads))
            delta = jnp.sum(jnp.where(mine, part, 0.0), axis=-1, keepdims=True)
            scores = mm(q_head, keys, 1, 1)
            soft = jnp.exp(scores - lse_ref[0, span, head : head + 1])
            soft = jnp.where(seen, soft, 0.0)
            back = mm(g_head, vals, 1, 1)
            score_grad = (soft * (back - delta)).astype(BF16)
            dq = mm(score_grad, keys, 1, 0)
            dk = mm(score_grad, q_head, 0, 0)
            dv = mm(soft.astype(BF16), g_head, 0, 0)
            if head == 0:
                dq_acc[span, :] = dq
            else:
                dq_acc[span, :] = jnp.where(mine, dq, dq_acc[span, :]) * HD**-0.5
            if head == 0 and number == 0:
                dk_acc[span, :] = dk
                dv_acc[span, :] = dv
            else:
                if head == 0:
                    if first:
                        dk_acc[0:first, :] += dk[:first]
                        dv_acc[0:first, :] += dv[:first]
                    dk_acc[span, :] = dk[first:]
                    dv_acc[span, :] = dv[first:]
                else:
                    dk_acc[0:length, :] += dk
                    dv_acc[0:length, :] += dv
    cosine = cos_ref[...]
    sine = sin_ref[...]
    grad_q = turn(dq_acc[...], cosine, sine, -1.0)
    grad_k = turn(dk_acc[...], cosine, sine, -1.0)
    grad_v = dv_acc[...]
    qb_ref[...] = jnp.concatenate(
        [jnp.sum(g, axis=0, keepdims=True) for g in (grad_q, grad_k, grad_v)]
        + [jnp.zeros((5, PAIR), F32)],
        0,
    )
    grad_q, grad_k, grad_v = (g.astype(BF16) for g in (grad_q, grad_k, grad_v))
    grads = jnp.concatenate([grad_q, grad_k, grad_v], 1)
    bit = bit_ref[0]
    here = pl.multiple_of(pair * PAIR, PAIR)
    for a_ref, b_ref, side in ((as_ref, bs_ref, 1 - bit), (ak_ref, bk_ref, bit)):
        cut = pl.ds(pl.multiple_of(side * half, PAIR), half)
        weight_grad = mm(attn_in_ref[:, cut], grads, 0, 0)
        a_ref[:, pl.ds(here, PAIR)] = weight_grad[:, :PAIR]
        a_ref[:, pl.ds(pl.multiple_of(half + here, PAIR), PAIR)] = weight_grad[:, PAIR : 2 * PAIR]
        b_ref[:, pl.ds(here, PAIR)] = weight_grad[:, 2 * PAIR :]
        b_ref[pl.ds(here, PAIR), half:] = mm(att_ref[...], gh_ref[:, cut], 0, 0)
    weights = jnp.concatenate([wq_ref[...], wk_ref[...], wv_ref[...]], 1)
    steps = pl.num_programs(0)
    first_sum = jnp.zeros((1, D), F32)
    second_sum = jnp.zeros((1, D), F32)
    for first in range(0, rows, BLOCK):
        span = pl.ds(first, BLOCK)
        added = mm(grads[first : first + BLOCK], weights, 1, 1)
        first_sum += jnp.sum(added * normed_ref[span, :], axis=0, keepdims=True)
        second_sum += jnp.sum(added, axis=0, keepdims=True)

        @pl.when(pair == 0)
        def _():
            e_ref[span, :] = em_ref[span, :] + added * ga_ref[...]

        @pl.when(pair > 0)
        def _():
            e_ref[span, :] += added * ga_ref[...]

    @pl.when(pair == 0)
    def _():
        sums_ref[...] = jnp.zeros_like(sums_ref)

    sums_ref[0:1, :] += first_sum
    sums_ref[1:2, :] += second_sum


def attention_backward(bit, attn_in, flat_qkv, cosine, sine, out_weight, gh, em, normed, ga, q, k, v, att, lse):
    rows = attn_in.shape[0]
    inner = out_weight.shape[0]
    pairs = inner // PAIR
    tall = (rows, D)
    half = (D // 2, 2 * inner)
    lane = pl.BlockSpec((rows, PAIR), lambda i, b: (0, i))
    return call(
        backward_kernel,
        (pairs,),
        [whole(tall)]
        + [slot_cols(s, D) for s in range(3)]
        + [whole((rows, PAIR)), whole((rows, PAIR)), pl.BlockSpec((PAIR, D), lambda i, b: (i, 0))]
        + [whole(tall), whole(tall), whole(tall), whole((1, D))]
        + [lane] * 4
        + [pl.BlockSpec((1, rows, 2), lambda i, b: (i, 0, 0))],
        [kept_out(tall)]
        + [kept_out(half)] * 4
        + [pl.BlockSpec((8, PAIR), lambda i, b: (0, i)), kept_out((8, D))],
        [sds(tall)] + [sds(half)] * 4 + [sds((8, inner)), sds((8, D))],
        [pltpu.VMEM((rows, PAIR), F32)] * 3,
        flops=14 * rows * D * inner + 10 * rows * rows * inner,
        nbytes=30_000_000,
    )(bit, attn_in, flat_qkv, flat_qkv, flat_qkv, cosine, sine, out_weight, gh, em, normed, ga, q, k, v, att, lse)


def rotary_tables(length):
    halfrot = ROT // 2
    frequency = jnp.exp(jnp.arange(halfrot, dtype=F32) * (-2.0 * math.log(10000.0) / ROT))
    angles = frequency[:, None] * jnp.arange(length, dtype=F32)[None, :]
    rest = ((0, HD - ROT), (0, 0))
    cosine = jnp.pad(jnp.tile(jnp.cos(angles), (2, 1)), rest, constant_values=1.0)
    sine = jnp.pad(jnp.tile(jnp.sin(angles), (2, 1)), rest)
    return jnp.tile(cosine, (2, 1)).T, jnp.tile(sine, (2, 1)).T


def assemble_kernel(bit_ref, own_ref, other_ref, whole_ref):
    mine = pl.program_id(0) == bit_ref[0]

    @pl.when(mine)
    def _():
        whole_ref[...] = own_ref[...]

    @pl.when(jnp.logical_not(mine))
    def _():
        whole_ref[...] = other_ref[...]


def assemble(bit, own, other, axis):
    height, width = own.shape
    rows = math.gcd(height, 192)
    count = height // rows

    def pick(mine, i, j, bit_ref):
        side = bit_ref[0] if mine else 1 - bit_ref[0]
        return jnp.where(i == side, j, jnp.where(i == 0, 0, count - 1)), 0

    place = (lambda i, j, b: (i * count + j, 0)) if axis == 0 else (lambda i, j, b: (j, i))
    return call(
        assemble_kernel,
        (2, count),
        [
            pl.BlockSpec((rows, width), lambda i, j, b: pick(True, i, j, b)),
            pl.BlockSpec((rows, width), lambda i, j, b: pick(False, i, j, b)),
        ],
        pl.BlockSpec((rows, width), place),
        sds((2 * height, width) if axis == 0 else (height, 2 * width)),
        nbytes=4 * height * width * 4,
    )(bit, own, other)


def attention_grads_kernel(bit_ref, a_own, a_other, b_own, b_other, qkv_ref, out_ref):
    half, inner = qkv_ref.shape[1] // 2, qkv_ref.shape[2]
    for side, a_ref, b_ref in ((bit_ref[0], a_own, b_own), (1 - bit_ref[0], a_other, b_other)):
        span = pl.ds(pl.multiple_of(side * half, PAIR), half)
        qkv_ref[0, span, :] = a_ref[:, :inner]
        qkv_ref[1, span, :] = a_ref[:, inner:]
        qkv_ref[2, span, :] = b_ref[:, :inner]
        out_ref[:, span] = b_ref[:, inner:]


def attention_grads(bit, a_own, a_other, b_own, b_other, inner):
    half = whole((D // 2, 2 * inner))
    return call(
        attention_grads_kernel,
        (1,),
        [half] * 4,
        [kept_out((3, D, inner)), kept_out((inner, D))],
        [sds((3, D, inner)), sds((inner, D))],
        nbytes=8 * D * 4 * inner,
    )(bit, a_own, a_other, b_own, b_other)


def input_grad_kernel(og_ref, mine_ref, other_ref, normed_ref, inv_ref, out_ref):
    shared = mine_ref[...] + other_ref[...]
    normed = normed_ref[...]
    mean = jnp.mean(shared, axis=-1, keepdims=True)
    along = jnp.mean(shared * normed, axis=-1, keepdims=True)
    out_ref[...] = og_ref[...] + inv_ref[...] * (shared - mean - normed * along)


def input_grad_of(og, mine, other, normed, inv_std):
    rows = og.shape[0]
    block = pl.BlockSpec((BLOCK, D), lambda i: (i, 0))
    return call(
        input_grad_kernel,
        (rows // BLOCK,),
        [block] * 4 + [pl.BlockSpec((BLOCK, 1), lambda i: (i, 0))],
        block,
        sds((rows, D)),
        nbytes=20 * rows * D,
        prefetch=0,
    )(og, mine, other, normed, inv_std)


def flip(axis, mask):
    return [(place, place ^ mask) for place in range(lax.axis_size(axis))]


def from_mask(rows, mask):
    return lax.ppermute(rows, "dp", flip("dp", mask))


def from_partner(rows):
    return lax.ppermute(rows, "tensor", flip("tensor", 1))


def give_half(rows, bit, mask):
    half = rows.shape[0] // 2
    sent = lax.dynamic_slice_in_dim(rows, (1 - bit) * half, half, 0)
    kept = lax.dynamic_slice_in_dim(rows, bit * half, half, 0)
    return kept + from_mask(sent, mask)


def join_half(rows, bit, mask):
    half = rows.shape[0]
    other = from_mask(rows, mask)
    joined = jnp.zeros((2 * half,) + rows.shape[1:], rows.dtype)
    joined = lax.dynamic_update_slice_in_dim(joined, rows, bit * half, 0)
    return lax.dynamic_update_slice_in_dim(joined, other, (1 - bit) * half, 0)


def sum_of_halves(send, keep, order):
    place = lax.axis_index("dp")
    rows = keep + from_mask(send, 1)
    stages = [((place >> k) & 1, 1 << k) for k in order]
    for bit, mask in stages[:-1]:
        rows = give_half(rows, bit, mask)
    for _, mask in stages[-1:]:
        rows = rows + from_mask(rows, mask)
    for bit, mask in reversed(stages[:-1]):
        rows = join_half(rows, bit, mask)
    return rows


def small_sum(rows):
    mask = 1
    while mask < lax.axis_size("dp"):
        rows = rows + from_mask(rows, mask)
        mask *= 2
    return rows


def on_device(
    block_input, gain_attn, bias_attn, gain_mlp, bias_mlp, qkv_weight, qkv_bias, out_weight, out_bias,
    up_weight, up_bias, down_weight, down_bias, out_grad,
):
    inner = out_weight.shape[0]
    bit = (lax.axis_index("dp") & 1).astype(jnp.int32).reshape(1)
    bits = lax.axis_size("dp").bit_length() - 1
    near = list(range(1, bits))
    far = near[1::-1] + near[2:]
    ga, ba, gm, bm = (v.reshape(1, D) for v in (gain_attn, bias_attn, gain_mlp, bias_mlp))
    weight = jnp.swapaxes(qkv_weight, 0, 1)
    cosine, sine = rotary_tables(L)
    (
        attn_in, gh, normed, inv_std, part, em, up_send, up_keep, down_send, down_keep, grad_up_b, mlp_sums,
    ) = mlp(bit, block_input, out_grad, ga, ba, gm, bm, up_weight, up_bias.reshape(1, -1), down_weight)
    q, k, v, att, lse, branches = attention_forward(
        attn_in, weight, qkv_bias[:, None, :], cosine, sine, part, out_weight
    )
    block_output = block_input + (branches + from_partner(branches)) + out_bias + down_bias
    shared, a_send, a_keep, b_send, b_keep, qkv_b, attn_sums = attention_backward(
        bit, attn_in, weight, cosine, sine, out_weight, gh, em, normed, ga, q, k, v, att, lse
    )
    input_grad = input_grad_of(out_grad, shared, from_partner(shared), normed, inv_std)

    norm_sums = jnp.concatenate([attn_sums[:2], mlp_sums[1:3]])
    norm_sums = norm_sums + from_partner(norm_sums)
    small = jnp.concatenate(
        [norm_sums.reshape(-1), qkv_b[:3].reshape(-1), grad_up_b.reshape(-1), mlp_sums[0]]
    ).reshape(-1, 128)
    small = small_sum(small).reshape(-1)
    cuts = [D, 2 * D, 3 * D, 4 * D, 4 * D + 3 * inner, 4 * D + 3 * inner + up_bias.shape[0]]
    gain_a, bias_a, gain_m, bias_m, qkv_b, up_b, out_b = jnp.split(small, cuts)

    up_own = sum_of_halves(up_send, up_keep, near)
    down_own = sum_of_halves(down_send, down_keep, far)
    grad_up = assemble(bit, up_own, from_mask(up_own, 1), 1)
    grad_down = assemble(bit, down_own, from_mask(down_own, 1), 0)
    a_own = sum_of_halves(a_send, a_keep, near)
    b_own = sum_of_halves(b_send, b_keep, far)
    grad_qkv, grad_out = attention_grads(bit, a_own, from_mask(a_own, 1), b_own, from_mask(b_own, 1), inner)
    return (
        block_output, input_grad, gain_a, bias_a, gain_m, bias_m, jnp.swapaxes(grad_qkv, 0, 1),
        qkv_b.reshape(3, inner), grad_out, out_b, grad_up, up_b, grad_down,
    )


def solution(mesh):
    in_specs = (
        P("dp", None),
        P(),
        P(),
        P(),
        P(),
        P(None, None, "tensor"),
        P(None, "tensor"),
        P("tensor", None),
        P(),
        P(None, "tensor"),
        P("tensor"),
        P("tensor", None),
        P(),
        P("dp", None),
    )
    out_specs = (
        P("dp", None),
        P("dp", None),
        P(),
        P(),
        P(),
        P(),
        P(None, None, "tensor"),
        P(None, "tensor"),
        P("tensor", None),
        P(),
        P(None, "tensor"),
        P("tensor"),
        P("tensor", None),
    )
    return jax.shard_map(
        on_device, mesh=mesh, in_specs=in_specs, out_specs=out_specs, check_vma=False
    )
```
